32 devices in a mesh: ad: 8 (over z, core), tp: 4 (over y, x).
Axes of the slice: x: 2, y: 2, z: 4, core: 2. Of those that a mesh axis runs over, the one named last changes fastest.
Arguments:
- tokens: bfloat16 [1024, 8192], P('ad', 'tp'), may hold values from -6 to 6
- query_weight: bfloat16 [8192, 8192], P(None, 'tp'), may hold values from -0.0625 to 0.0625
- adapter_down_weight: bfloat16 [128, 8192, 64], P('ad', 'tp'), may hold values from -0.0625 to 0.0625
- adapter_up_weight: bfloat16 [128, 64, 8192], P('ad', None, 'tp'), may hold values from -0.75 to 0.75
- row_adapter_index: int32 [1024], P('ad'), may hold values from 0 to 127, as said below
- adapter_table_slot: int32 [128], replicated, may hold values from 0 to 127, as said below
- lengths: int32 [1024], P('ad'), may hold values from 1 to 64, as said below
- cached_key_rows: bfloat16 [1024, 8, 64, 128], P('ad', None, 'tp'), may hold values from -360 to 360
- cached_value_rows: bfloat16 [1024, 8, 64, 128], P('ad', None, 'tp'), may hold values from -6 to 6
Outputs:
- queries: bfloat16 [1024, 8192], P('ad', 'tp')
- attended: bfloat16 [1024, 8192], P('ad', 'tp')
The draws below stay inside these ranges and needn't reach their ends.
Inputs may be any that keep to these rules, and one draw needn't show every extreme that they name: `row_adapter_index`: within each aligned block of 128 rows at most 48 rows have their adapter's slot in any one run of 16 slots (slot // 16); one such run, drawn from the seed, is named by exactly 48 rows of every block. `adapter_table_slot`: A permutation of the slots. `lengths`: some row has exactly 64 and some row exactly 1.
All inputs are finite; a program needn't handle non-finite values.
Results may differ from the reference program's by a relative error of at most 0.019.
Values may be sent and summed in bfloat16 or wider, within the bound.
A program may use at most 128 MiB of HBM per device.

```python
import math
import jax
import jax.numpy as jnp
from jax import lax

MODEL_WIDTH = 8192
QUERY_HEADS = 64
KVH = 8
HEAD_SIZE = 128
ADAPTER_RANK = 64
ADAPT_DEV = 16
ROWS_DEV = 128
POS_DEV = 16
ADAPTER_TOTAL = 128
ROWS = 1024
CTX = 64
CAP = 48
N_TP = 4


def owner_table(key):
    return jax.random.permutation(jax.random.fold_in(key, 11), ADAPTER_TOTAL).astype(jnp.int32)


def draw_adapter_table_slot(key, part):
    return owner_table(key)


def draw_row_adapter_index(key, part):
    table = owner_table(key)
    inverse = jnp.argsort(table, stable=True).astype(jnp.int32)
    blocks = ROWS // ROWS_DEV
    hottest = jax.random.randint(jax.random.fold_in(key, 12), (), 0, blocks).astype(jnp.int32)
    pool_size = (blocks - 1) * CAP

    def one_block(index):
        inner = jax.random.fold_in(jax.random.fold_in(key, 13), index)
        picks = jax.random.permutation(jax.random.fold_in(inner, 1), pool_size)[:ROWS_DEV - CAP].astype(jnp.int32)
        others = picks // CAP
        others = others + (others >= hottest).astype(jnp.int32)
        owners = jnp.concatenate([jnp.full((CAP,), 0, jnp.int32) + hottest, others])
        owners = jax.random.permutation(jax.random.fold_in(inner, 2), owners)
        local_partial = jax.random.randint(jax.random.fold_in(inner, 3), (ROWS_DEV,), 0, ADAPT_DEV).astype(jnp.int32)
        return inverse[owners * ADAPT_DEV + local_partial]
    return jax.vmap(one_block)(jnp.arange(blocks, dtype=jnp.int32)).reshape(ROWS).astype(jnp.int32)


def draw_lengths(key, part):
    values = jax.random.randint(jax.random.fold_in(key, 21), (ROWS,), 1, CTX + 1).astype(jnp.int32)
    longest = jax.random.randint(jax.random.fold_in(key, 22), (), 0, ROWS // 2)
    shortest = jax.random.randint(jax.random.fold_in(key, 23), (), ROWS // 2, ROWS)
    values = values.at[longest].set(CTX)
    return values.at[shortest].set(1)


def draw_cached_key_rows(key, part):
    values = jax.random.normal(jax.random.fold_in(key, 31), (ROWS, KVH, CTX, HEAD_SIZE), jnp.float32)
    values = jnp.clip(values, -6.0, 6.0)
    return values.astype(jnp.bfloat16)


def levels(rng, extent, cuts, least, largest):
    def one(dim, shards_of):
        steps = jax.random.uniform(jax.random.fold_in(jax.random.fold_in(rng, 6), dim), (shards_of,), jnp.float32, least / len(cuts), largest / len(cuts))
        return jnp.repeat(jnp.exp(steps), extent[dim] // shards_of).reshape((-1,) + (1,) * (len(extent) - dim - 1))

    factor_of = one(*cuts[0])
    for cut in cuts[1:]:
        factor_of = factor_of * one(*cut)
    return factor_of


def gaussian(own_key, dims, deviation, most, pieces=(), kind=jnp.bfloat16):
    loudness = levels(own_key, dims, pieces, -0.22, 0.18) if pieces else 1.0
    values = jax.random.normal(own_key, dims, jnp.float32) * deviation * loudness
    return jnp.minimum(jnp.maximum(values, -most), most).astype(kind)


def setup_inputs(seed: int = 0) -> dict:
    key_of = jax.random.split(jax.random.key(seed), 10)
    return {
        "tokens": gaussian(key_of[0], (ROWS, MODEL_WIDTH), 1.0, 6.0, ((0, 8), (1, 4))),
        "query_weight": gaussian(key_of[1], (MODEL_WIDTH, QUERY_HEADS * HEAD_SIZE), MODEL_WIDTH ** -0.5, 0.0625, ((1, 4),)),
        "adapter_down_weight": gaussian(key_of[2], (ADAPTER_TOTAL, MODEL_WIDTH, ADAPTER_RANK), MODEL_WIDTH ** -0.5, 0.0625, ((0, 8), (1, 4))),
        "adapter_up_weight": gaussian(key_of[3], (ADAPTER_TOTAL, ADAPTER_RANK, QUERY_HEADS * HEAD_SIZE), ADAPTER_RANK ** -0.5, 0.75, ((0, 8), (2, 4))),
        "row_adapter_index": draw_row_adapter_index(jax.random.fold_in(key_of[9], 71), 0),
        "adapter_table_slot": draw_adapter_table_slot(jax.random.fold_in(key_of[9], 71), 0),
        "lengths": draw_lengths(jax.random.fold_in(key_of[9], 71), 0),
        "cached_key_rows": draw_cached_key_rows(jax.random.fold_in(key_of[9], 71), 0),
        "cached_value_rows": gaussian(key_of[8], (ROWS, KVH, CTX, HEAD_SIZE), 1.0, 6.0, ((0, 8), (2, 4))),
    }


def rotate(query, lengths):
    head_dim = query.shape[-1]
    half = head_dim // 2
    freq = jnp.exp(jnp.arange(half, dtype=jnp.float32) * (-2.0 * math.log(500000.0) / head_dim))
    angle = (lengths - 1).astype(jnp.float32)[:, None, None] * freq[None, None, :]
    cosine = jnp.cos(angle)
    sine = jnp.sin(angle)
    first = query[..., :half]
    second = query[..., half:]
    return jnp.concatenate([first * cosine - second * sine, second * cosine + first * sine], axis=-1)

def reference(tokens, query_weight, adapter_down_weight, adapter_up_weight, row_adapter_index, adapter_table_slot, lengths, cached_key_rows, cached_value_rows):
    base = jnp.dot(tokens, query_weight, preferred_element_type=jnp.float32)
    slots = adapter_table_slot[row_adapter_index]

    def adapter_block(input_rows):
        rows, slot_row_table = input_rows
        down_weight = adapter_down_weight[slot_row_table].astype(jnp.float32)
        reduced_rows = jnp.einsum('rd,rdk->rk', rows.astype(jnp.float32), down_weight).astype(jnp.bfloat16)
        up_weight = adapter_up_weight[slot_row_table].astype(jnp.float32)
        return jnp.einsum('rk,rke->re', reduced_rows.astype(jnp.float32), up_weight).astype(jnp.bfloat16)
    delta = lax.map(adapter_block, (tokens.reshape(ROWS // 64, 64, MODEL_WIDTH), slots.reshape(ROWS // 64, 64)))
    delta = delta.reshape(ROWS, QUERY_HEADS * HEAD_SIZE)
    query = (base + delta.astype(jnp.float32)).reshape(ROWS, QUERY_HEADS, HEAD_SIZE)
    queries = rotate(query, lengths).reshape(ROWS, QUERY_HEADS * HEAD_SIZE).astype(jnp.bfloat16)
    scale = 1.0 / math.sqrt(HEAD_SIZE)
    group = QUERY_HEADS // KVH

    def attend_block(input_rows):
        qrows, keys, values, lens = input_rows
        grouped = qrows.reshape(64, KVH, group, HEAD_SIZE).astype(jnp.float32)
        keys = keys.reshape(64, KVH, N_TP, POS_DEV, HEAD_SIZE).astype(jnp.float32)
        values = values.reshape(64, KVH, N_TP, POS_DEV, HEAD_SIZE).astype(jnp.float32)
        scores = jnp.einsum('rkgd,rkbpd->rkgbp', grouped, keys) * scale
        position = jnp.arange(CTX, dtype=jnp.int32).reshape(N_TP, POS_DEV)
        valid = (position[None, :, :] < lens[:, None, None])[:, None, None, :, :]
        scores = jnp.where(valid, scores, -1e+30)
        peak = lax.optimization_barrier(jnp.max(scores, axis=-1))
        weights = jnp.where(valid, jnp.exp(scores - peak[..., None]), 0.0)
        total = lax.optimization_barrier(jnp.sum(weights, axis=-1))
        partial_value_sum = jnp.einsum('rkgbp,rkbpd->rkgbd', weights.astype(jnp.bfloat16).astype(jnp.float32), values).astype(jnp.bfloat16)
        top = lax.optimization_barrier(jnp.max(peak, axis=-1, keepdims=True))
        factor = jnp.exp(peak - top)
        numer = lax.optimization_barrier(jnp.sum(factor[..., None] * partial_value_sum.astype(jnp.float32), axis=3))
        denom = lax.optimization_barrier(jnp.sum(factor * total, axis=3))
        return (numer / denom[..., None]).reshape(64, QUERY_HEADS * HEAD_SIZE).astype(jnp.bfloat16)
    attended = lax.map(attend_block, (queries.reshape(ROWS // 64, 64, QUERY_HEADS * HEAD_SIZE), cached_key_rows.reshape(ROWS // 64, 64, KVH, CTX, HEAD_SIZE), cached_value_rows.reshape(ROWS // 64, 64, KVH, CTX, HEAD_SIZE), lengths.reshape(ROWS // 64, 64)))
    return (queries, attended.reshape(ROWS, QUERY_HEADS * HEAD_SIZE))
```

```python
import functools
import math

import jax
import jax.numpy as jnp
from jax import lax
from jax.experimental import pallas as pl
from jax.experimental.pallas import tpu as pltpu
from jax.sharding import PartitionSpec as P

MESH = pl.DeviceIdType.MESH
LANES = 128


def remote(src, dst, send_sem, recv_sem, axis, peer):
    return pltpu.make_async_remote_copy(
        src_ref=src,
        dst_ref=dst,
        send_sem=send_sem,
        recv_sem=recv_sem,
        device_id={axis: peer},
        device_id_type=MESH,
    )


def greet(counts):
    barrier = pltpu.get_barrier_semaphore()
    total = 0
    for axis, count in counts:
        me = lax.axis_index(axis)
        for d in range(1, count):
            pl.semaphore_signal(
                barrier, inc=1, device_id={axis: lax.rem(me + d, count)}, device_id_type=MESH
            )
            total += 1
    pl.semaphore_wait(barrier, total)


def query_kernel(
    n_ad,
    n_tp,
    cap,
    rank,
    packed_ref,
    unpack_ref,
    tokens_ref,
    cos_ref,
    sin_ref,
    weight_hbm,
    down_hbm,
    up_hbm,
    out_ref,
    gathered,
    arrived,
    outgoing,
    returned,
    part_send,
    part_recv,
    acc,
    weight_buf,
    down_buf,
    down_wide,
    up_buf,
    weight_sem,
    down_sem,
    up_sem,
    tok_send,
    tok_recv,
    row_send,
    row_recv,
    sum_send,
    sum_recv,
    ret_send,
    ret_recv,
):
    ad = lax.axis_index("ad")
    tp = lax.axis_index("tp")
    features = tokens_ref.shape[1]
    columns = out_ref.shape[1]
    depth = weight_buf.shape[1]
    slots = weight_buf.shape[0]
    subs = features // depth
    steps = n_tp * subs
    per = LANES // rank
    wide = down_wide.shape[2]
    tiles = down_wide.shape[0]
    groups = n_ad // 2
    rows2 = 2 * cap

    def weight_copy(i):
        owner = lax.rem(tp + n_tp - i // subs, n_tp)
        start = pl.multiple_of(owner * features + (i % subs) * depth, depth)
        return pltpu.make_async_copy(
            weight_hbm.at[pl.ds(start, depth), :], weight_buf.at[i % slots], weight_sem.at[i % slots]
        )

    pairs = down_buf.shape[0] // 2
    down_copies = [
        pltpu.make_async_copy(
            down_hbm.at[pl.ds(2 * j, 2)], down_buf.at[pl.ds(2 * j, 2)], down_sem.at[j]
        )
        for j in range(pairs)
    ]
    for copy in down_copies:
        copy.start()
    for i in range(slots):
        weight_copy(i).start()
    up_copy = pltpu.make_async_copy(up_hbm, up_buf, up_sem)
    up_copy.start()

    greet((("ad", n_ad), ("tp", n_tp)))

    row_copies = []
    for d in range(1, n_ad):
        peer = lax.rem(ad + d, n_ad)
        copy = remote(
            packed_ref.at[peer], arrived.at[d], row_send.at[d], row_recv.at[d], "ad", peer
        )
        copy.start()
        row_copies.append(copy)
    tok_copies = []
    for e in range(1, n_tp):
        copy = remote(
            tokens_ref, gathered.at[e], tok_send.at[e], tok_recv.at[e], "tp", lax.rem(tp + e, n_tp)
        )
        copy.start()
        tok_copies.append(copy)
    arrived[0] = packed_ref[ad]

    per_tile = wide // LANES
    for j in range(pairs):
        down_copies[j].wait()

        @pl.loop(0, features // 256)
        def _(c):
            at = pl.ds(pl.multiple_of(c * 256, 256), 256)
            down_wide[j // per_tile, at, pl.ds((j % per_tile) * LANES, LANES)] = jnp.concatenate(
                [down_buf[2 * j, at, :], down_buf[2 * j + 1, at, :]], axis=1
            )

    def base_chunk(e):
        if e:
            tok_copies[e - 1].wait_recv()
        block = tokens_ref if e == 0 else gathered.at[e]
        for sub in range(subs):
            i = e * subs + sub
            weight_copy(i).wait()

            @pl.loop(0, columns // 256)
            def _(c):
                at = pl.ds(pl.multiple_of(c * 256, 256), 256)
                product = jnp.dot(
                    block[:, pl.ds(sub * depth, depth)],
                    weight_buf[i % slots, :, at],
                    preferred_element_type=jnp.float32,
                )
                if i == 0:
                    acc[:, at] = product
                else:
                    acc[:, at] += product

            if i + slots < steps:
                weight_copy(i + slots).start()

    lane2 = lax.broadcasted_iota(jnp.int32, (rows2, LANES), 1)
    part_of = (lane2 // rank).astype(jnp.float32)
    lane1 = lax.broadcasted_iota(jnp.int32, (cap, LANES), 1)
    sum_copies = {}
    ret_copies = []

    def ids_of(g):
        return (
            arrived[pl.ds(2 * g, 2), :, pl.ds(features, LANES)]
            .reshape(rows2, LANES)
            .astype(jnp.float32)
            - 1.0
        )

    def shrink(g):
        for d in (2 * g, 2 * g + 1):
            if d:
                row_copies[d - 1].wait_recv()
        ids = ids_of(g) - part_of

        def tile(t, total):
            product = jnp.dot(
                arrived[pl.ds(2 * g, 2), :, pl.ds(0, features)].reshape(rows2, features),
                down_wide[t],
                preferred_element_type=jnp.float32,
            )
            for k in range(per_tile):
                want = ((t * per_tile + k) * per).astype(jnp.float32)
                total = total + jnp.where(
                    ids == want, product[:, k * LANES : (k + 1) * LANES], 0.0
                )
            return total

        total = lax.fori_loop(0, tiles, tile, jnp.zeros((rows2, LANES), jnp.float32))
        total = total + pltpu.roll(total, rank, 1)
        part_send[g] = jnp.where(lane1 < rank, total[:cap], total[cap:])
        for e in range(1, n_tp):
            copy = remote(
                part_send.at[g],
                part_recv.at[g, e],
                sum_send.at[g, e],
                sum_recv.at[g, e],
                "tp",
                lax.rem(tp + e, n_tp),
            )
            copy.start()
            sum_copies[g, e] = copy

    def expand(g):
        if g == 0:
            up_copy.wait()
        total = part_send[g]
        for e in range(1, n_tp):
            sum_copies[g, e].wait_recv()
            total = total + part_recv[g, e]
        turned = pltpu.roll(total, rank, 1)
        both = jnp.concatenate(
            [jnp.where(lane1 < rank, total, turned), jnp.where(lane1 < rank, turned, total)], axis=0
        )
        ids = ids_of(g) - part_of
        spread = jnp.concatenate(
            [jnp.where(ids == float(j * per), both, 0.0).astype(jnp.bfloat16) for j in range(pairs)],
            axis=1,
        )

        @pl.loop(0, columns // 256)
        def _(c):
            at = pl.ds(pl.multiple_of(c * 256, 256), 256)
            change = jnp.dot(spread, up_buf[:, at], preferred_element_type=jnp.float32)
            outgoing[pl.ds(2 * g, 2), :, at] = change.astype(jnp.bfloat16).reshape(2, cap, 256)

        for d in (2 * g, 2 * g + 1):
            if d:
                copy = remote(
                    outgoing.at[d],
                    returned.at[ad],
                    ret_send.at[d],
                    ret_recv.at[d],
                    "ad",
                    lax.rem(ad + n_ad - d, n_ad),
                )
                copy.start()
                ret_copies.append(copy)
            else:
                returned[ad] = outgoing[0]

    shrink(0)
    base_chunk(0)
    expand(0)
    for g in range(1, groups):
        shrink(g)
        if g < n_tp:
            base_chunk(g)
        expand(g)
    for e in range(groups, n_tp):
        base_chunk(e)
    for copy in ret_copies:
        copy.wait_recv()

    head = cos_ref.shape[1]

    @pl.loop(0, columns // 256)
    def _(c):
        at = pl.ds(pl.multiple_of(c * 256, 256), 256)
        delta = jnp.dot(
            unpack_ref[...],
            returned[:, :, at].reshape(n_ad * cap, 256),
            preferred_element_type=jnp.float32,
        )
        query = acc[:, at] + delta
        pieces = []
        for h in range(256 // head):
            one = query[:, h * head : (h + 1) * head]
            pieces.append(one * cos_ref[...] + pltpu.roll(one, head // 2, 1) * sin_ref[...])
        out_ref[:, at] = jnp.concatenate(pieces, axis=1).astype(jnp.bfloat16)

    for copy in row_copies + tok_copies + list(sum_copies.values()) + ret_copies:
        copy.wait_send()


def attend_kernel(
    n_tp,
    chunk,
    span,
    kv_heads,
    lengths_ref,
    queries_ref,
    keys_hbm,
    values_hbm,
    out_ref,
    every,
    keys,
    values,
    part,
    stat,
    part_in,
    stat_in,
    key_sem,
    value_sem,
    q_send,
    q_recv,
    p_send,
    p_recv,
    s_send,
    s_recv,
):
    tp = lax.axis_index("tp")
    rows, heads, size = queries_ref.shape
    chunks = rows // chunk
    all_heads = n_tp * heads
    cells = kv_heads * span
    scale = 1.0 / math.sqrt(size)
    loads = []
    for c in range(chunks):
        at = pl.ds(c * chunk, chunk)
        pair = (
            pltpu.make_async_copy(keys_hbm.at[at], keys.at[at], key_sem.at[c]),
            pltpu.make_async_copy(values_hbm.at[at], values.at[at], value_sem.at[c]),
        )
        for copy in pair:
            copy.start()
        loads.append(pair)
    greet((("tp", n_tp),))
    sends = {}
    for c in range(chunks):
        at = pl.ds(c * chunk, chunk)
        for e in range(1, n_tp):
            copy = remote(
                queries_ref.at[at],
                every.at[tp, at],
                q_send.at[c, e],
                q_recv.at[c, e],
                "tp",
                lax.rem(tp + e, n_tp),
            )
            copy.start()
            sends[c, e] = copy
    every[tp] = queries_ref[...]

    head_of = lax.broadcasted_iota(jnp.int32, (all_heads, cells), 0) // (all_heads // kv_heads)
    cell = lax.broadcasted_iota(jnp.int32, (all_heads, cells), 1)
    mine = head_of == cell // span
    position = jnp.where(mine, tp * span + cell % span, 1 << 30)
    lane = lax.broadcasted_iota(jnp.int32, (all_heads, LANES), 1)
    lane_h = lax.broadcasted_iota(jnp.int32, (heads, LANES), 1)
    unroll = 4
    outs = []

    def attend(c):
        for copy in loads[c]:
            copy.wait()
        for e in range(1, n_tp):
            sends[c, e].wait_recv()

        def some(b, held):
            for u in range(unroll):
                local = b * unroll + u
                r = c * chunk + local
                query = jnp.concatenate([every[t, r] for t in range(n_tp)], axis=0)
                score = (
                    lax.dot_general(
                        query, keys[r], (((1,), (1,)), ((), ())), preferred_element_type=jnp.float32
                    )
                    * scale
                )
                valid = position < lengths_ref[r]
                score = jnp.where(valid, score, -1e30)
                peak = jnp.max(score, axis=1, keepdims=True)
                weight = jnp.where(valid, jnp.exp(score - peak), 0.0)
                total = jnp.sum(weight, axis=1, keepdims=True)
                result = jnp.dot(
                    weight.astype(jnp.bfloat16), values[r], preferred_element_type=jnp.float32
                ).astype(jnp.bfloat16)
                for t in range(n_tp):
                    part[t, r] = result[t * heads : (t + 1) * heads]
                held = jnp.where(lane == local, peak, held)
                held = jnp.where(lane == local + LANES // 2, total, held)
            return held

        held = lax.fori_loop(
            0, chunk // unroll, some, jnp.zeros((all_heads, LANES), jnp.float32)
        )
        for t in range(n_tp):
            stat[c, t] = held[t * heads : (t + 1) * heads]
        at = pl.ds(c * chunk, chunk)
        for e in range(1, n_tp):
            peer = lax.rem(tp + e, n_tp)
            p = remote(
                part.at[peer, at], part_in.at[e, at], p_send.at[c, e], p_recv.at[c, e], "tp", peer
            )
            s = remote(
                stat.at[c, peer], stat_in.at[c, e], s_send.at[c, e], s_recv.at[c, e], "tp", peer
            )
            s.start()
            p.start()
            outs.append((c, s))
            outs.append((c, p))
        part_in[0, at] = part[tp, at]
        stat_in[c, 0] = stat[c, tp]

    def combine(c):
        for k, copy in outs:
            if k == c:
                copy.wait_recv()
        stats = [stat_in[c, e] for e in range(n_tp)]
        top = functools.reduce(jnp.maximum, stats)
        factors = [jnp.exp(s - top) for s in stats]
        denom = sum(f * pltpu.roll(s, LANES // 2, 1) for f, s in zip(factors, stats))
        shares = [f / denom for f in factors]

        @pl.loop(0, chunk // unroll)
        def _(b):
            for u in range(unroll):
                local = b * unroll + u
                r = c * chunk + local
                result = jnp.zeros((heads, size), jnp.float32)
                for e in range(n_tp):
                    share = jnp.sum(
                        jnp.where(lane_h == local, shares[e], 0.0), axis=1, keepdims=True
                    )
                    result = result + share * part_in[e, r].astype(jnp.float32)
                out_ref[r] = result.astype(jnp.bfloat16)

    for c in range(chunks):
        attend(c)
        if c:
            combine(c - 1)
    combine(chunks - 1)
    for copy in list(sends.values()) + [copy for _, copy in outs]:
        copy.wait_send()


def fused_device(
    tokens,
    query_weight,
    adapter_down_weight,
    adapter_up_weight,
    row_adapter_index,
    adapter_table_slot,
    lengths,
    cached_key_rows,
    cached_value_rows,
):
    rows, features = tokens.shape
    columns = query_weight.shape[1]
    n_ad = lax.axis_size("ad")
    n_tp = lax.axis_size("tp")
    held = adapter_down_weight.shape[0]
    rank = adapter_down_weight.shape[2]
    _, kv_heads, span, head_dim = cached_key_rows.shape
    cap = -(-(384 // n_ad) // 16) * 16

    slots = lookup(row_adapter_index, adapter_table_slot)
    owner = slots // held
    order = jnp.arange(rows, dtype=jnp.int32)
    before = (owner[:, None] == owner[None, :]) & (order[None, :] < order[:, None])
    place = owner * cap + jnp.sum(before.astype(jnp.int32), axis=1)
    cells = jnp.arange(n_ad * cap, dtype=jnp.int32)
    pack = (cells[:, None] == place[None, :]).astype(jnp.bfloat16)
    unpack = (place[:, None] == cells[None, :]).astype(jnp.bfloat16)
    marked = jnp.concatenate(
        [
            tokens,
            jnp.broadcast_to((slots % held + 1).astype(jnp.bfloat16)[:, None], (rows, LANES)),
        ],
        axis=1,
    )
    packed = jnp.dot(pack, marked, preferred_element_type=jnp.float32).astype(jnp.bfloat16)
    packed = packed.reshape(n_ad, cap, features + LANES)

    half = head_dim // 2
    freq = jnp.exp(jnp.arange(half, dtype=jnp.float32) * (-2.0 * math.log(500000.0) / head_dim))
    angle = (lengths - 1).astype(jnp.float32)[:, None] * freq[None, :]
    cosine = jnp.cos(angle)
    sine = jnp.sin(angle)
    cos_full = jnp.concatenate([cosine, cosine], axis=1)
    sin_full = jnp.concatenate([-sine, sine], axis=1)

    depth = 1024
    slot_count = 4
    vmem = pl.BlockSpec(memory_space=pltpu.VMEM)
    anywhere = pl.BlockSpec(memory_space=pl.ANY)
    bf16, f32 = jnp.bfloat16, jnp.float32
    dma = pltpu.SemaphoreType.DMA
    groups = n_ad // 2
    queries = pl.pallas_call(
        functools.partial(query_kernel, n_ad, n_tp, cap, rank),
        out_shape=jax.ShapeDtypeStruct((rows, columns), bf16),
        in_specs=[vmem] * 5 + [anywhere] * 3,
        out_specs=vmem,
        scratch_shapes=[
            pltpu.VMEM((n_tp, rows, features), bf16),
            pltpu.VMEM((n_ad, cap, features + LANES), bf16),
            pltpu.VMEM((n_ad, cap, columns), bf16),
            pltpu.VMEM((n_ad, cap, columns), bf16),
            pltpu.VMEM((groups, cap, LANES), f32),
            pltpu.VMEM((groups, n_tp, cap, LANES), f32),
            pltpu.VMEM((rows, columns), f32),
            pltpu.VMEM((slot_count, depth, columns), bf16),
            pltpu.VMEM((held, features, rank), bf16),
            pltpu.VMEM((held * rank // 256, features, 256), bf16),
            pltpu.VMEM((held * rank, columns), bf16),
            dma((slot_count,)),
            dma((held // 2,)),
            dma,
            dma((n_tp,)),
            dma((n_tp,)),
            dma((n_ad,)),
            dma((n_ad,)),
            dma((groups, n_tp)),
            dma((groups, n_tp)),
            dma((n_ad,)),
            dma((n_ad,)),
        ],
        compiler_params=pltpu.CompilerParams(
            collective_id=0, has_side_effects=True, vmem_limit_bytes=60 * 1024 * 1024
        ),
        name="project",
    )(
        packed,
        unpack,
        tokens,
        cos_full,
        sin_full,
        query_weight,
        adapter_down_weight,
        adapter_up_weight.reshape(held * rank, columns),
    )

    heads = columns // head_dim
    chunk = 32
    chunks = rows // chunk
    attended = pl.pallas_call(
        functools.partial(attend_kernel, n_tp, chunk, span, kv_heads),
        out_shape=jax.ShapeDtypeStruct((rows, heads, head_dim), bf16),
        in_specs=[pl.BlockSpec(memory_space=pltpu.SMEM), vmem] + [anywhere] * 2,
        out_specs=vmem,
        scratch_shapes=[
            pltpu.VMEM((n_tp, rows, heads, head_dim), bf16),
            pltpu.VMEM((rows, kv_heads * span, head_dim), bf16),
            pltpu.VMEM((rows, kv_heads * span, head_dim), bf16),
            pltpu.VMEM((n_tp, rows, heads, head_dim), bf16),
            pltpu.VMEM((chunks, n_tp, heads, LANES), f32),
            pltpu.VMEM((n_tp, rows, heads, head_dim), bf16),
            pltpu.VMEM((chunks, n_tp, heads, LANES), f32),
            dma((chunks,)),
            dma((chunks,)),
            dma((chunks, n_tp)),
            dma((chunks, n_tp)),
            dma((chunks, n_tp)),
            dma((chunks, n_tp)),
            dma((chunks, n_tp)),
            dma((chunks, n_tp)),
        ],
        compiler_params=pltpu.CompilerParams(
            collective_id=1, has_side_effects=True, vmem_limit_bytes=48 * 1024 * 1024
        ),
        name="attend",
    )(
        lengths,
        queries.reshape(rows, heads, head_dim),
        cached_key_rows.reshape(rows, kv_heads * span, head_dim),
        cached_value_rows.reshape(rows, kv_heads * span, head_dim),
    )
    return (queries, attended.reshape(rows, columns))


def rotate(query, lengths):
    head_dim = query.shape[-1]
    half = head_dim // 2
    freq = jnp.exp(jnp.arange(half, dtype=jnp.float32) * (-2.0 * math.log(500000.0) / head_dim))
    angle = (lengths - 1).astype(jnp.float32)[:, None, None] * freq[None, None, :]
    cosine = jnp.cos(angle)
    sine = jnp.sin(angle)
    first = query[..., :half]
    second = query[..., half:]
    return jnp.concatenate(
        [first * cosine - second * sine, second * cosine + first * sine], axis=-1
    )


def lookup(ids, adapter_table_slot):
    table = jnp.arange(adapter_table_slot.shape[0], dtype=jnp.int32)
    return jnp.sum(
        jnp.where(ids[:, None] == table[None, :], adapter_table_slot[None, :], 0), axis=1
    )


def shrink_rows(input_rows, local_partial, adapter_down_weight):
    adapter_row_count = adapter_down_weight.shape[0]
    select_rows = (
        local_partial[:, None] == jnp.arange(adapter_row_count, dtype=jnp.int32)[None, :]
    ).astype(jnp.float32)
    update_terms = jnp.einsum(
        "nt,vtm->nvm", input_rows, adapter_down_weight, preferred_element_type=jnp.float32
    )
    return (select_rows, jnp.sum(update_terms * select_rows[:, :, None], axis=1))


def expand_rows(select_rows, reduced_rows, adapter_up_weight):
    spread_rows = (select_rows[:, :, None] * reduced_rows.astype(jnp.float32)[:, None, :]).astype(
        jnp.bfloat16
    )
    return jnp.einsum(
        "pow,owu->pu", spread_rows, adapter_up_weight, preferred_element_type=jnp.float32
    ).astype(jnp.bfloat16)


def per_device(
    tokens,
    query_weight,
    adapter_down_weight,
    adapter_up_weight,
    row_adapter_index,
    adapter_table_slot,
    lengths,
    cached_key_rows,
    cached_value_rows,
):
    rows = tokens.shape[0]
    columns = query_weight.shape[1]
    tp_count = lax.axis_size("tp")
    owner_partials = adapter_down_weight.shape[0]
    base = jnp.dot(
        lax.all_gather(tokens, "tp", axis=1, tiled=True),
        query_weight,
        preferred_element_type=jnp.float32,
    )
    combined_output, every_id = (
        lax.all_gather(tokens, "ad", axis=0, tiled=True),
        lax.all_gather(row_adapter_index, "ad", axis=0, tiled=True),
    )
    slots = lookup(every_id, adapter_table_slot)
    mine = slots // owner_partials == lax.axis_index("ad")
    local_partial = jnp.where(mine, slots % owner_partials, -1)
    select_rows, partial_value_sum = shrink_rows(
        combined_output, local_partial, adapter_down_weight
    )
    reduced_rows = lax.psum(partial_value_sum, "tp").astype(jnp.bfloat16)
    lowrank_change = expand_rows(select_rows, reduced_rows, adapter_up_weight)
    delta = lax.psum_scatter(
        lowrank_change.astype(jnp.float32).astype(jnp.bfloat16),
        "ad",
        scatter_dimension=0,
        tiled=True,
    ).astype(jnp.float32)
    head_dim = cached_key_rows.shape[3]
    query = (base + delta).reshape(rows, columns // head_dim, head_dim)
    queries = rotate(query, lengths).reshape(rows, columns).astype(jnp.bfloat16)
    every_head = lax.all_gather(queries, "tp", axis=1, tiled=True)
    kv_heads = cached_key_rows.shape[1]
    span = cached_key_rows.shape[2]
    grouped = every_head.reshape(rows, kv_heads, -1, head_dim)
    scores = jnp.einsum(
        "rkgd,rkpd->rkgp", grouped, cached_key_rows, preferred_element_type=jnp.float32
    ) * (1.0 / math.sqrt(head_dim))
    position = lax.axis_index("tp") * span + jnp.arange(span, dtype=jnp.int32)
    valid = (position[None, :] < lengths[:, None])[:, None, None, :]
    scores = jnp.where(valid, scores, -1e30)
    peak = jnp.max(scores, axis=-1)
    weights = jnp.where(valid, jnp.exp(scores - peak[..., None]), 0.0)
    total = jnp.sum(weights, axis=-1)
    partial_out = jnp.einsum(
        "rkgp,rkpd->rkgd",
        weights.astype(jnp.bfloat16),
        cached_value_rows,
        preferred_element_type=jnp.float32,
    ).astype(jnp.bfloat16)
    peaks, totals = (
        lax.all_to_all(
            peak.reshape(rows, tp_count, -1), "tp", split_axis=1, concat_axis=1, tiled=True
        ),
        lax.all_to_all(
            total.reshape(rows, tp_count, -1), "tp", split_axis=1, concat_axis=1, tiled=True
        ),
    )
    partials = lax.all_to_all(
        partial_out.reshape(rows, tp_count, -1), "tp", split_axis=1, concat_axis=1, tiled=True
    )
    highest = jnp.max(peaks, axis=1, keepdims=True)
    factor = jnp.exp(peaks - highest)
    numer = jnp.sum(
        factor[..., None] * partials.reshape(rows, tp_count, -1, head_dim).astype(jnp.float32),
        axis=1,
    )
    denom = jnp.sum(factor * totals, axis=1)
    attended = (numer / denom[..., None]).reshape(rows, columns).astype(jnp.bfloat16)
    return (queries, attended)


def solution(mesh):
    fits = mesh.shape["tp"] <= 4 and mesh.shape["ad"] % 2 == 0
    return jax.shard_map(
        fused_device if fits else per_device,
        mesh=mesh,
        in_specs=(
            P("ad", "tp"),
            P(None, "tp"),
            P("ad", "tp", None),
            P("ad", None, "tp"),
            P("ad"),
            P(),
            P("ad"),
            P("ad", None, "tp", None),
            P("ad", None, "tp", None),
        ),
        out_specs=(P("ad", "tp"), P("ad", "tp")),
        check_vma=False,
    )
```

```python
import functools
import math

import jax
import jax.numpy as jnp
from jax import lax
from jax.experimental import pallas as pl
from jax.experimental.pallas import tpu as pltpu
from jax.sharding import PartitionSpec as P

MESH = pl.DeviceIdType.MESH
LANES = 128
SWAPPED = 64


def remote(src, dst, send_sem, recv_sem, axis, peer):
    return pltpu.make_async_remote_copy(
        src_ref=src,
        dst_ref=dst,
        send_sem=send_sem,
        recv_sem=recv_sem,
        device_id={axis: peer},
        device_id_type=MESH,
    )


def greet(counts):
    barrier = pltpu.get_barrier_semaphore()
    total = 0
    for axis, count in counts:
        me = lax.axis_index(axis)
        for d in range(1, count):
            pl.semaphore_signal(
                barrier, inc=1, device_id={axis: lax.rem(me + d, count)}, device_id_type=MESH
            )
            total += 1
    pl.semaphore_wait(barrier, total)


def step_kernel(
    n_ad,
    n_tp,
    cap,
    rank,
    swapped,
    chunk,
    place_ref,
    mark_ref,
    unpack_ref,
    tokens_ref,
    cos_ref,
    sin_ref,
    lengths_ref,
    weight_hbm,
    down_hbm,
    up_hbm,
    keys_hbm,
    values_hbm,
    out_ref,
    att_ref,
    packed,
    gathered,
    arrived,
    outgoing,
    returned,
    part_send,
    part_recv,
    acc,
    weight_buf,
    down_buf,
    up_buf,
    heads_f32,
    heads_bf16,
    swap_keys,
    swap_values,
    every,
    keys,
    values,
    part,
    stat,
    part_in,
    stat_in,
    weight_sem,
    load_sem,
    tok_send,
    tok_recv,
    row_send,
    row_recv,
    sum_send,
    sum_recv,
    ret_send,
    ret_recv,
    swap_send,
    swap_recv,
    q_send,
    q_recv,
    p_send,
    p_recv,
    s_send,
    s_recv,
):
    ad = lax.axis_index("ad")
    tp = lax.axis_index("tp")
    rows, features = tokens_ref.shape
    columns = out_ref.shape[1]
    depth = weight_buf.shape[1]
    slots = weight_buf.shape[0]
    subs = features // depth
    steps = n_tp * subs
    per = LANES // rank
    pairs = down_buf.shape[0] // LANES
    tiles = down_buf.shape[0] // 256
    per_tile = 256 // LANES
    groups = n_ad // 2
    rows2 = 2 * cap
    heads, size = heads_bf16.shape[1:]
    kv_heads, span = keys_hbm.shape[1:3]
    kv_mine = kv_heads // n_tp
    spread_rows = rows - swapped
    chunks = spread_rows // chunk
    all_heads = n_tp * heads
    cells = kv_heads * span
    scale = 1.0 / math.sqrt(size)

    def weight_copy(i):
        owner = lax.rem(tp + n_tp - i // subs, n_tp)
        start = pl.multiple_of(owner * features + (i % subs) * depth, depth)
        return pltpu.make_async_copy(
            weight_hbm.at[pl.ds(start, depth), :], weight_buf.at[i % slots], weight_sem.at[i % slots]
        )

    down_copy = pltpu.make_async_copy(down_hbm, down_buf, load_sem.at[0])
    up_copy = pltpu.make_async_copy(up_hbm, up_buf, load_sem.at[1])
    down_copy.start()
    for i in range(slots):
        weight_copy(i).start()
    up_copy.start()
    early = pl.ds(0, swapped)
    late = pl.ds(swapped, spread_rows)
    own_kv = pl.ds(tp * kv_mine, kv_mine)
    cache_copies = [
        pltpu.make_async_copy(keys_hbm.at[early, own_kv], swap_keys.at[:, 0], load_sem.at[2]),
        pltpu.make_async_copy(values_hbm.at[early, own_kv], swap_values.at[:, 0], load_sem.at[3]),
        pltpu.make_async_copy(keys_hbm.at[late], keys, load_sem.at[4]),
        pltpu.make_async_copy(values_hbm.at[late], values, load_sem.at[5]),
    ]

    greet((("ad", n_ad), ("tp", n_tp)))

    tok_copies = []
    for e in range(1, n_tp):
        copy = remote(
            tokens_ref, gathered.at[e], tok_send.at[e], tok_recv.at[e], "tp", lax.rem(tp + e, n_tp)
        )
        copy.start()
        tok_copies.append(copy)

    cell_row = lax.broadcasted_iota(jnp.int32, (cap, rows), 0)

    def pack_into(d, peer, target):
        pick = (cell_row + peer * cap == place_ref[...]).astype(jnp.bfloat16)

        @pl.loop(0, features // 512)
        def _(c):
            at = pl.ds(pl.multiple_of(c * 512, 512), 512)
            target[d, :, at] = jnp.dot(
                pick, tokens_ref[:, at], preferred_element_type=jnp.float32
            ).astype(jnp.bfloat16)

        target[d, :, pl.ds(features, LANES)] = jnp.dot(
            pick, mark_ref[...], preferred_element_type=jnp.float32
        ).astype(jnp.bfloat16)

    row_copies = []
    for d in range(1, n_ad):
        peer = lax.rem(ad + d, n_ad)
        pack_into(d, peer, packed)
        copy = remote(packed.at[d], arrived.at[d], row_send.at[d], row_recv.at[d], "ad", peer)
        copy.start()
        row_copies.append(copy)
    pack_into(0, ad, arrived)

    swap_copies = []

    def swap(which, source, target):
        for e in range(1, n_tp):
            peer = lax.rem(tp + e, n_tp)
            copy = remote(
                source.at[early, pl.ds(peer * kv_mine, kv_mine)],
                target.at[:, e],
                swap_send.at[which, e],
                swap_recv.at[which, e],
                "tp",
                peer,
            )
            copy.start()
            swap_copies.append(copy)

    def base_chunk(e):
        if e:
            tok_copies[e - 1].wait_recv()
        block = tokens_ref if e == 0 else gathered.at[e]
        for sub in range(subs):
            i = e * subs + sub
            weight_copy(i).wait()

            @pl.loop(0, columns // 256)
            def _(c):
                at = pl.ds(pl.multiple_of(c * 256, 256), 256)
                product = jnp.dot(
                    block[:, pl.ds(sub * depth, depth)],
                    weight_buf[i % slots, :, at],
                    preferred_element_type=jnp.float32,
                )
                if i == 0:
                    acc[:, at] = product
                else:
                    acc[:, at] += product

            if i + slots < steps:
                weight_copy(i + slots).start()

    lane2 = lax.broadcasted_iota(jnp.int32, (rows2, LANES), 1)
    part_of = (lane2 // rank).astype(jnp.float32)
    lane1 = lax.broadcasted_iota(jnp.int32, (cap, LANES), 1)
    sum_copies = {}
    ret_copies = []

    def ids_of(g):
        return (
            arrived[pl.ds(2 * g, 2), :, pl.ds(features, LANES)]
            .reshape(rows2, LANES)
            .astype(jnp.float32)
            - 1.0
        )

    def shrink(g):
        for d in (2 * g, 2 * g + 1):
            if d:
                row_copies[d - 1].wait_recv()
        if g == 0:
            down_copy.wait()
        ids = ids_of(g) - part_of

        def tile(t, total):
            product = lax.dot_general(
                arrived[pl.ds(2 * g, 2), :, pl.ds(0, features)].reshape(rows2, features),
                down_buf[pl.ds(pl.multiple_of(t * 256, 256), 256), :],
                (((1,), (1,)), ((), ())),
                preferred_element_type=jnp.float32,
            )
            for k in range(per_tile):
                want = ((t * per_tile + k) * per).astype(jnp.float32)
                total = total + jnp.where(
                    ids == want, product[:, k * LANES : (k + 1) * LANES], 0.0
                )
            return total

        total = lax.fori_loop(0, tiles, tile, jnp.zeros((rows2, LANES), jnp.float32))
        total = total + pltpu.roll(total, rank, 1)
        part_send[g] = jnp.where(lane1 < rank, total[:cap], total[cap:])
        for e in range(1, n_tp):
            copy = remote(
                part_send.at[g],
                part_recv.at[g, e],
                sum_send.at[g, e],
                sum_recv.at[g, e],
                "tp",
                lax.rem(tp + e, n_tp),
            )
            copy.start()
            sum_copies[g, e] = copy

    def expand(g):
        if g == 0:
            up_copy.wait()
        total = part_send[g]
        for e in range(1, n_tp):
            sum_copies[g, e].wait_recv()
            total = total + part_recv[g, e]
        turned = pltpu.roll(total, rank, 1)
        both = jnp.concatenate(
            [jnp.where(lane1 < rank, total, turned), jnp.where(lane1 < rank, turned, total)], axis=0
        )
        ids = ids_of(g) - part_of
        spread = jnp.concatenate(
            [jnp.where(ids == float(j * per), both, 0.0).astype(jnp.bfloat16) for j in range(pairs)],
            axis=1,
        )

        @pl.loop(0, columns // 256)
        def _(c):
            at = pl.ds(pl.multiple_of(c * 256, 256), 256)
            change = jnp.dot(spread, up_buf[:, at], preferred_element_type=jnp.float32)
            outgoing[pl.ds(2 * g, 2), :, at] = change.astype(jnp.bfloat16).reshape(2, cap, 256)

        for d in (2 * g, 2 * g + 1):
            if d:
                copy = remote(
                    outgoing.at[d],
                    returned.at[ad],
                    ret_send.at[d],
                    ret_recv.at[d],
                    "ad",
                    lax.rem(ad + n_ad - d, n_ad),
                )
                copy.start()
                ret_copies.append(copy)
            else:
                returned[ad] = outgoing[0]

    swap(0, keys_hbm, swap_keys)
    shrink(0)
    base_chunk(0)
    expand(0)
    for copy in cache_copies:
        copy.start()
    for g in range(1, groups):
        shrink(g)
        if g < n_tp:
            base_chunk(g)
        expand(g)
    swap(1, values_hbm, swap_values)
    for e in range(groups, n_tp):
        base_chunk(e)
    for copy in ret_copies:
        copy.wait_recv()

    @pl.loop(0, columns // 256)
    def _(c):
        at = pl.ds(pl.multiple_of(c * 256, 256), 256)
        delta = jnp.dot(
            unpack_ref[...],
            returned[:, :, at].reshape(n_ad * cap, 256),
            preferred_element_type=jnp.float32,
        )
        query = acc[:, at] + delta
        pieces = []
        for h in range(256 // size):
            one = query[:, h * size : (h + 1) * size]
            pieces.append(one * cos_ref[...] + pltpu.roll(one, size // 2, 1) * sin_ref[...])
        out_ref[:, at] = jnp.concatenate(pieces, axis=1).astype(jnp.bfloat16)

    for h in range(heads):
        heads_f32[:, h, :] = out_ref[:, h * size : (h + 1) * size].astype(jnp.float32)
    heads_bf16[...] = heads_f32[...].astype(jnp.bfloat16)

    sends = {}
    for c in range(chunks):
        for e in range(1, n_tp):
            copy = remote(
                heads_bf16.at[pl.ds(swapped + c * chunk, chunk)],
                every.at[tp, pl.ds(c * chunk, chunk)],
                q_send.at[c, e],
                q_recv.at[c, e],
                "tp",
                lax.rem(tp + e, n_tp),
            )
            copy.start()
            sends[c, e] = copy
    every[tp] = heads_bf16[pl.ds(swapped, spread_rows)]

    for copy in swap_copies:
        copy.wait_recv()
    for copy in cache_copies:
        copy.wait()

    own_head = lax.broadcasted_iota(jnp.int32, (heads, cells), 0) // (heads // kv_mine)
    own_cell = lax.broadcasted_iota(jnp.int32, (heads, cells), 1)
    block = kv_mine * span
    own_mine = own_head == (own_cell % block) // span
    source = lax.rem(tp + n_tp - own_cell // block, n_tp)
    own_position = jnp.where(own_mine, source * span + own_cell % span, 1 << 30)

    @pl.loop(0, swapped // 8)
    def _(b):
        for u in range(8):
            r = b * 8 + u
            score = (
                lax.dot_general(
                    heads_bf16[r],
                    swap_keys[r].reshape(cells, size),
                    (((1,), (1,)), ((), ())),
                    preferred_element_type=jnp.float32,
                )
                * scale
            )
            valid = own_position < lengths_ref[r]
            score = jnp.where(valid, score, -1e30)
            peak = jnp.max(score, axis=1, keepdims=True)
            weight = jnp.where(valid, jnp.exp(score - peak), 0.0)
            total = jnp.sum(weight, axis=1, keepdims=True)
            result = jnp.dot(
                weight.astype(jnp.bfloat16),
                swap_values[r].reshape(cells, size),
                preferred_element_type=jnp.float32,
            )
            heads_f32[r] = result / total

    head_of = lax.broadcasted_iota(jnp.int32, (all_heads, cells), 0) // (all_heads // kv_heads)
    cell = lax.broadcasted_iota(jnp.int32, (all_heads, cells), 1)
    mine = head_of == cell // span
    position = jnp.where(mine, tp * span + cell % span, 1 << 30)
    lane = lax.broadcasted_iota(jnp.int32, (all_heads, LANES), 1)
    lane_h = lax.broadcasted_iota(jnp.int32, (heads, LANES), 1)
    unroll = 4
    outs = []

    def attend(c):
        for e in range(1, n_tp):
            sends[c, e].wait_recv()

        def some(b, held):
            for u in range(unroll):
                local = b * unroll + u
                r = c * chunk + local
                query = jnp.concatenate([every[t, r] for t in range(n_tp)], axis=0)
                score = (
                    lax.dot_general(
                        query,
                        keys[r].reshape(cells, size),
                        (((1,), (1,)), ((), ())),
                        preferred_element_type=jnp.float32,
                    )
                    * scale
                )
                valid = position < lengths_ref[swapped + r]
                score = jnp.where(valid, score, -1e30)
                peak = jnp.max(score, axis=1, keepdims=True)
                weight = jnp.where(valid, jnp.exp(score - peak), 0.0)
                total = jnp.sum(weight, axis=1, keepdims=True)
                result = jnp.dot(
                    weight.astype(jnp.bfloat16),
                    values[r].reshape(cells, size),
                    preferred_element_type=jnp.float32,
                ).astype(jnp.bfloat16)
                for t in range(n_tp):
                    part[t, r] = result[t * heads : (t + 1) * heads]
                held = jnp.where(lane == local, peak, held)
                held = jnp.where(lane == local + LANES // 2, total, held)
            return held

        held = lax.fori_loop(
            0, chunk // unroll, some, jnp.zeros((all_heads, LANES), jnp.float32)
        )
        for t in range(n_tp):
            stat[c, t] = held[t * heads : (t + 1) * heads]
        at = pl.ds(c * chunk, chunk)
        for e in range(1, n_tp):
            peer = lax.rem(tp + e, n_tp)
            s = remote(
                stat.at[c, peer], stat_in.at[c, e], s_send.at[c, e], s_recv.at[c, e], "tp", peer
            )
            p = remote(
                part.at[peer, at], part_in.at[e, at], p_send.at[c, e], p_recv.at[c, e], "tp", peer
            )
            s.start()
            p.start()
            outs.append((c, s))
            outs.append((c, p))
        part_in[0, at] = part[tp, at]
        stat_in[c, 0] = stat[c, tp]

    def combine(c):
        for k, copy in outs:
            if k == c:
                copy.wait_recv()
        stats = [stat_in[c, e] for e in range(n_tp)]
        top = functools.reduce(jnp.maximum, stats)
        factors = [jnp.exp(s - top) for s in stats]
        denom = sum(f * pltpu.roll(s, LANES // 2, 1) for f, s in zip(factors, stats))
        shares = [f / denom for f in factors]

        @pl.loop(0, chunk // unroll)
        def _(b):
            for u in range(unroll):
                local = b * unroll + u
                r = c * chunk + local
                result = jnp.zeros((heads, size), jnp.float32)
                for e in range(n_tp):
                    share = jnp.sum(
                        jnp.where(lane_h == local, shares[e], 0.0), axis=1, keepdims=True
                    )
                    result = result + share * part_in[e, r].astype(jnp.float32)
                heads_f32[swapped + r] = result

    for c in range(chunks):
        attend(c)
        if c:
            combine(c - 1)
    combine(chunks - 1)
    for h in range(heads):
        att_ref[:, h * size : (h + 1) * size] = heads_f32[:, h, :].astype(jnp.bfloat16)

    for copy in row_copies + tok_copies + list(sum_copies.values()) + ret_copies:
        copy.wait_send()
    for copy in swap_copies + list(sends.values()) + [copy for _, copy in outs]:
        copy.wait_send()


def fused_device(
    tokens,
    query_weight,
    adapter_down_weight,
    adapter_up_weight,
    row_adapter_index,
    adapter_table_slot,
    lengths,
    cached_key_rows,
    cached_value_rows,
):
    rows, features = tokens.shape
    columns = query_weight.shape[1]
    n_ad = lax.axis_size("ad")
    n_tp = lax.axis_size("tp")
    held = adapter_down_weight.shape[0]
    rank = adapter_down_weight.shape[2]
    _, kv_heads, span, head_dim = cached_key_rows.shape
    cap = -(-(384 // n_ad) // 16) * 16

    slots = lookup(row_adapter_index, adapter_table_slot)
    owner = slots // held
    order = jnp.arange(rows, dtype=jnp.int32)
    before = (owner[:, None] == owner[None, :]) & (order[None, :] < order[:, None])
    place = owner * cap + jnp.sum(before.astype(jnp.int32), axis=1)
    cells = jnp.arange(n_ad * cap, dtype=jnp.int32)
    unpack = (place[:, None] == cells[None, :]).astype(jnp.bfloat16)
    mark = jnp.broadcast_to((slots % held + 1).astype(jnp.bfloat16)[:, None], (rows, LANES))

    half = head_dim // 2
    freq = jnp.exp(jnp.arange(half, dtype=jnp.float32) * (-2.0 * math.log(500000.0) / head_dim))
    angle = (lengths - 1).astype(jnp.float32)[:, None] * freq[None, :]
    cosine = jnp.cos(angle)
    sine = jnp.sin(angle)
    cos_full = jnp.concatenate([cosine, cosine], axis=1)
    sin_full = jnp.concatenate([-sine, sine], axis=1)

    depth = 1024
    slot_count = 4
    swapped = SWAPPED
    chunk = 32
    heads = columns // head_dim
    spread_rows = rows - swapped
    chunks = spread_rows // chunk
    kv_mine = kv_heads // n_tp
    vmem = pl.BlockSpec(memory_space=pltpu.VMEM)
    smem = pl.BlockSpec(memory_space=pltpu.SMEM)
    anywhere = pl.BlockSpec(memory_space=pl.ANY)
    bf16, f32 = jnp.bfloat16, jnp.float32
    dma = pltpu.SemaphoreType.DMA
    groups = n_ad // 2
    return pl.pallas_call(
        functools.partial(step_kernel, n_ad, n_tp, cap, rank, swapped, chunk),
        out_shape=(jax.ShapeDtypeStruct((rows, columns), bf16),) * 2,
        in_specs=[vmem] * 6 + [smem] + [anywhere] * 5,
        out_specs=(vmem, vmem),
        scratch_shapes=[
            pltpu.VMEM((n_ad, cap, features + LANES), bf16),
            pltpu.VMEM((n_tp, rows, features), bf16),
            pltpu.VMEM((n_ad, cap, features + LANES), bf16),
            pltpu.VMEM((n_ad, cap, columns), bf16),
            pltpu.VMEM((n_ad, cap, columns), bf16),
            pltpu.VMEM((groups, cap, LANES), f32),
            pltpu.VMEM((groups, n_tp, cap, LANES), f32),
            pltpu.VMEM((rows, columns), f32),
            pltpu.VMEM((slot_count, depth, columns), bf16),
            pltpu.VMEM((held * rank, features), bf16),
            pltpu.VMEM((held * rank, columns), bf16),
            pltpu.VMEM((rows, heads, head_dim), f32),
            pltpu.VMEM((rows, heads, head_dim), bf16),
            pltpu.VMEM((swapped, n_tp, kv_mine, span, head_dim), bf16),
            pltpu.VMEM((swapped, n_tp, kv_mine, span, head_dim), bf16),
            pltpu.VMEM((n_tp, spread_rows, heads, head_dim), bf16),
            pltpu.VMEM((spread_rows, kv_heads, span, head_dim), bf16),
            pltpu.VMEM((spread_rows, kv_heads, span, head_dim), bf16),
            pltpu.VMEM((n_tp, spread_rows, heads, head_dim), bf16),
            pltpu.VMEM((chunks, n_tp, heads, LANES), f32),
            pltpu.VMEM((n_tp, spread_rows, heads, head_dim), bf16),
            pltpu.VMEM((chunks, n_tp, heads, LANES), f32),
            dma((slot_count,)),
            dma((6,)),
            dma((n_tp,)),
            dma((n_tp,)),
            dma((n_ad,)),
            dma((n_ad,)),
            dma((groups, n_tp)),
            dma((groups, n_tp)),
            dma((n_ad,)),
            dma((n_ad,)),
            dma((2, n_tp)),
            dma((2, n_tp)),
            dma((chunks, n_tp)),
            dma((chunks, n_tp)),
            dma((chunks, n_tp)),
            dma((chunks, n_tp)),
            dma((chunks, n_tp)),
            dma((chunks, n_tp)),
        ],
        compiler_params=pltpu.CompilerParams(
            collective_id=0, has_side_effects=True, vmem_limit_bytes=60 * 1024 * 1024
        ),
        name="step",
    )(
        place[None, :],
        mark,
        unpack,
        tokens,
        cos_full,
        sin_full,
        lengths,
        query_weight,
        adapter_down_weight.transpose(0, 2, 1).reshape(held * rank, features),
        adapter_up_weight.reshape(held * rank, columns),
        cached_key_rows,
        cached_value_rows,
    )


def rotate(query, lengths):
    head_dim = query.shape[-1]
    half = head_dim // 2
    freq = jnp.exp(jnp.arange(half, dtype=jnp.float32) * (-2.0 * math.log(500000.0) / head_dim))
    angle = (lengths - 1).astype(jnp.float32)[:, None, None] * freq[None, None, :]
    cosine = jnp.cos(angle)
    sine = jnp.sin(angle)
    first = query[..., :half]
    second = query[..., half:]
    return jnp.concatenate(
        [first * cosine - second * sine, second * cosine + first * sine], axis=-1
    )


def lookup(ids, adapter_table_slot):
    table = jnp.arange(adapter_table_slot.shape[0], dtype=jnp.int32)
    return jnp.sum(
        jnp.where(ids[:, None] == table[None, :], adapter_table_slot[None, :], 0), axis=1
    )


def shrink_rows(input_rows, local_partial, adapter_down_weight):
    adapter_row_count = adapter_down_weight.shape[0]
    select_rows = (
        local_partial[:, None] == jnp.arange(adapter_row_count, dtype=jnp.int32)[None, :]
    ).astype(jnp.float32)
    update_terms = jnp.einsum(
        "nt,vtm->nvm", input_rows, adapter_down_weight, preferred_element_type=jnp.float32
    )
    return (select_rows, jnp.sum(update_terms * select_rows[:, :, None], axis=1))


def expand_rows(select_rows, reduced_rows, adapter_up_weight):
    spread_rows = (select_rows[:, :, None] * reduced_rows.astype(jnp.float32)[:, None, :]).astype(
        jnp.bfloat16
    )
    return jnp.einsum(
        "pow,owu->pu", spread_rows, adapter_up_weight, preferred_element_type=jnp.float32
    ).astype(jnp.bfloat16)


def per_device(
    tokens,
    query_weight,
    adapter_down_weight,
    adapter_up_weight,
    row_adapter_index,
    adapter_table_slot,
    lengths,
    cached_key_rows,
    cached_value_rows,
):
    rows = tokens.shape[0]
    columns = query_weight.shape[1]
    tp_count = lax.axis_size("tp")
    owner_partials = adapter_down_weight.shape[0]
    base = jnp.dot(
        lax.all_gather(tokens, "tp", axis=1, tiled=True),
        query_weight,
        preferred_element_type=jnp.float32,
    )
    combined_output, every_id = (
        lax.all_gather(tokens, "ad", axis=0, tiled=True),
        lax.all_gather(row_adapter_index, "ad", axis=0, tiled=True),
    )
    slots = lookup(every_id, adapter_table_slot)
    mine = slots // owner_partials == lax.axis_index("ad")
    local_partial = jnp.where(mine, slots % owner_partials, -1)
    select_rows, partial_value_sum = shrink_rows(
        combined_output, local_partial, adapter_down_weight
    )
    reduced_rows = lax.psum(partial_value_sum, "tp").astype(jnp.bfloat16)
    lowrank_change = expand_rows(select_rows, reduced_rows, adapter_up_weight)
    delta = lax.psum_scatter(
        lowrank_change.astype(jnp.float32).astype(jnp.bfloat16),
        "ad",
        scatter_dimension=0,
        tiled=True,
    ).astype(jnp.float32)
    head_dim = cached_key_rows.shape[3]
    query = (base + delta).reshape(rows, columns // head_dim, head_dim)
    queries = rotate(query, lengths).reshape(rows, columns).astype(jnp.bfloat16)
    every_head = lax.all_gather(queries, "tp", axis=1, tiled=True)
    kv_heads = cached_key_rows.shape[1]
    span = cached_key_rows.shape[2]
    grouped = every_head.reshape(rows, kv_heads, -1, head_dim)
    scores = jnp.einsum(
        "rkgd,rkpd->rkgp", grouped, cached_key_rows, preferred_element_type=jnp.float32
    ) * (1.0 / math.sqrt(head_dim))
    position = lax.axis_index("tp") * span + jnp.arange(span, dtype=jnp.int32)
    valid = (position[None, :] < lengths[:, None])[:, None, None, :]
    scores = jnp.where(valid, scores, -1e30)
    peak = jnp.max(scores, axis=-1)
    weights = jnp.where(valid, jnp.exp(scores - peak[..., None]), 0.0)
    total = jnp.sum(weights, axis=-1)
    partial_out = jnp.einsum(
        "rkgp,rkpd->rkgd",
        weights.astype(jnp.bfloat16),
        cached_value_rows,
        preferred_element_type=jnp.float32,
    ).astype(jnp.bfloat16)
    peaks, totals = (
        lax.all_to_all(
            peak.reshape(rows, tp_count, -1), "tp", split_axis=1, concat_axis=1, tiled=True
        ),
        lax.all_to_all(
            total.reshape(rows, tp_count, -1), "tp", split_axis=1, concat_axis=1, tiled=True
        ),
    )
    partials = lax.all_to_all(
        partial_out.reshape(rows, tp_count, -1), "tp", split_axis=1, concat_axis=1, tiled=True
    )
    highest = jnp.max(peaks, axis=1, keepdims=True)
    factor = jnp.exp(peaks - highest)
    numer = jnp.sum(
        factor[..., None] * partials.reshape(rows, tp_count, -1, head_dim).astype(jnp.float32),
        axis=1,
    )
    denom = jnp.sum(factor * totals, axis=1)
    attended = (numer / denom[..., None]).reshape(rows, columns).astype(jnp.bfloat16)
    return (queries, attended)


def solution(mesh):
    fits = mesh.shape["tp"] <= 4 and mesh.shape["ad"] % 2 == 0
    return jax.shard_map(
        fused_device if fits else per_device,
        mesh=mesh,
        in_specs=(
            P("ad", "tp"),
            P(None, "tp"),
            P("ad", "tp", None),
            P("ad", None, "tp"),
            P("ad"),
            P(),
            P("ad"),
            P("ad", None, "tp", None),
            P("ad", None, "tp", None),
        ),
        out_specs=(P("ad", "tp"), P("ad", "tp")),
        check_vma=False,
    )
```

```python
import functools
import math

import jax
import jax.numpy as jnp
from jax import lax
from jax.experimental import pallas as pl
from jax.experimental.pallas import tpu as pltpu
from jax.sharding import PartitionSpec as P

MESH = pl.DeviceIdType.MESH
LANES = 128
SWAPPED = 32


def remote(src, dst, send_sem, recv_sem, axis, peer):
    return pltpu.make_async_remote_copy(
        src_ref=src,
        dst_ref=dst,
        send_sem=send_sem,
        recv_sem=recv_sem,
        device_id={axis: peer},
        device_id_type=MESH,
    )


def greet(counts):
    barrier = pltpu.get_barrier_semaphore()
    total = 0
    for axis, count in counts:
        me = lax.axis_index(axis)
        for d in range(1, count):
            pl.semaphore_signal(
                barrier, inc=1, device_id={axis: lax.rem(me + d, count)}, device_id_type=MESH
            )
            total += 1
    pl.semaphore_wait(barrier, total)


def step_kernel(
    n_ad,
    n_tp,
    cap,
    rank,
    swapped,
    chunk,
    place_ref,
    mark_ref,
    unpack_ref,
    tokens_ref,
    cos_ref,
    sin_ref,
    lengths_ref,
    weight_hbm,
    down_hbm,
    up_hbm,
    keys_hbm,
    values_hbm,
    out_ref,
    att_ref,
    packed,
    gathered,
    arrived,
    outgoing,
    returned,
    part_send,
    part_recv,
    acc,
    weight_buf,
    down_buf,
    up_buf,
    heads_f32,
    heads_bf16,
    swap_keys,
    swap_values,
    every,
    keys,
    values,
    part,
    stat,
    part_in,
    stat_in,
    weight_sem,
    load_sem,
    tok_send,
    tok_recv,
    row_send,
    row_recv,
    sum_send,
    sum_recv,
    ret_send,
    ret_recv,
    swap_send,
    swap_recv,
    q_send,
    q_recv,
    p_send,
    p_recv,
    s_send,
    s_recv,
):
    ad = lax.axis_index("ad")
    tp = lax.axis_index("tp")
    rows, features = tokens_ref.shape
    columns = out_ref.shape[1]
    depth = weight_buf.shape[1]
    slots = weight_buf.shape[0]
    subs = features // depth
    steps = n_tp * subs
    per = LANES // rank
    pairs = down_buf.shape[0] // LANES
    tiles = down_buf.shape[0] // 256
    per_tile = 256 // LANES
    groups = n_ad // 2
    rows2 = 2 * cap
    heads, size = heads_bf16.shape[1:]
    kv_heads, span = keys_hbm.shape[1:3]
    kv_mine = kv_heads // n_tp
    spread_rows = rows - swapped
    chunks = spread_rows // chunk
    all_heads = n_tp * heads
    cells = kv_heads * span
    scale = 1.0 / math.sqrt(size)

    def weight_copy(i):
        owner = lax.rem(tp + n_tp - i // subs, n_tp)
        start = pl.multiple_of(owner * features + (i % subs) * depth, depth)
        return pltpu.make_async_copy(
            weight_hbm.at[pl.ds(start, depth), :], weight_buf.at[i % slots], weight_sem.at[i % slots]
        )

    down_copy = pltpu.make_async_copy(down_hbm, down_buf, load_sem.at[0])
    up_copy = pltpu.make_async_copy(up_hbm, up_buf, load_sem.at[1])
    down_copy.start()
    for i in range(slots):
        weight_copy(i).start()
    up_copy.start()
    early = pl.ds(0, swapped)
    late = pl.ds(swapped, spread_rows)
    own_kv = pl.ds(tp * kv_mine, kv_mine)
    cache_copies = [
        pltpu.make_async_copy(keys_hbm.at[early, own_kv], swap_keys.at[:, 0], load_sem.at[2]),
        pltpu.make_async_copy(values_hbm.at[early, own_kv], swap_values.at[:, 0], load_sem.at[3]),
        pltpu.make_async_copy(keys_hbm.at[late], keys, load_sem.at[4]),
        pltpu.make_async_copy(values_hbm.at[late], values, load_sem.at[5]),
    ]

    greet((("ad", n_ad), ("tp", n_tp)))

    tok_copies = []
    for e in range(1, n_tp):
        copy = remote(
            tokens_ref, gathered.at[e], tok_send.at[e], tok_recv.at[e], "tp", lax.rem(tp + e, n_tp)
        )
        copy.start()
        tok_copies.append(copy)

    cell_row = lax.broadcasted_iota(jnp.int32, (cap, rows), 0)

    def pack_into(d, peer, target):
        pick = (cell_row + peer * cap == place_ref[...]).astype(jnp.bfloat16)

        @pl.loop(0, features // 512)
        def _(c):
            at = pl.ds(pl.multiple_of(c * 512, 512), 512)
            target[d, :, at] = jnp.dot(
                pick, tokens_ref[:, at], preferred_element_type=jnp.float32
            ).astype(jnp.bfloat16)

        target[d, :, pl.ds(features, LANES)] = jnp.dot(
            pick, mark_ref[...], preferred_element_type=jnp.float32
        ).astype(jnp.bfloat16)

    row_copies = []
    for d in range(1, n_ad):
        peer = lax.rem(ad + d, n_ad)
        pack_into(d, peer, packed)
        copy = remote(packed.at[d], arrived.at[d], row_send.at[d], row_recv.at[d], "ad", peer)
        copy.start()
        row_copies.append(copy)
    pack_into(0, ad, arrived)

    swap_copies = []

    def swap(which, source, target):
        for e in range(1, n_tp):
            peer = lax.rem(tp + e, n_tp)
            copy = remote(
                source.at[early, pl.ds(peer * kv_mine, kv_mine)],
                target.at[:, e],
                swap_send.at[which, e],
                swap_recv.at[which, e],
                "tp",
                peer,
            )
            copy.start()
            swap_copies.append(copy)

    def base_chunk(e):
        if e:
            tok_copies[e - 1].wait_recv()
        block = tokens_ref if e == 0 else gathered.at[e]
        for sub in range(subs):
            i = e * subs + sub
            weight_copy(i).wait()

            @pl.loop(0, columns // 256)
            def _(c):
                at = pl.ds(pl.multiple_of(c * 256, 256), 256)
                product = jnp.dot(
                    block[:, pl.ds(sub * depth, depth)],
                    weight_buf[i % slots, :, at],
                    preferred_element_type=jnp.float32,
                )
                if i == 0:
                    acc[:, at] = product
                else:
                    acc[:, at] += product

            if i + slots < steps:
                weight_copy(i + slots).start()

    lane2 = lax.broadcasted_iota(jnp.int32, (rows2, LANES), 1)
    part_of = (lane2 // rank).astype(jnp.float32)
    lane1 = lax.broadcasted_iota(jnp.int32, (cap, LANES), 1)
    sum_copies = {}
    ret_copies = []

    def ids_of(g):
        return (
            arrived[pl.ds(2 * g, 2), :, pl.ds(features, LANES)]
            .reshape(rows2, LANES)
            .astype(jnp.float32)
            - 1.0
        )

    def shrink(g):
        for d in (2 * g, 2 * g + 1):
            if d:
                row_copies[d - 1].wait_recv()
        if g == 0:
            down_copy.wait()
        ids = ids_of(g) - part_of

        def tile(t, total):
            product = lax.dot_general(
                arrived[pl.ds(2 * g, 2), :, pl.ds(0, features)].reshape(rows2, features),
                down_buf[pl.ds(pl.multiple_of(t * 256, 256), 256), :],
                (((1,), (1,)), ((), ())),
                preferred_element_type=jnp.float32,
            )
            for k in range(per_tile):
                want = ((t * per_tile + k) * per).astype(jnp.float32)
                total = total + jnp.where(
                    ids == want, product[:, k * LANES : (k + 1) * LANES], 0.0
                )
            return total

        total = lax.fori_loop(0, tiles, tile, jnp.zeros((rows2, LANES), jnp.float32))
        total = total + pltpu.roll(total, rank, 1)
        part_send[g] = jnp.where(lane1 < rank, total[:cap], total[cap:])
        for e in range(1, n_tp):
            copy = remote(
                part_send.at[g],
                part_recv.at[g, e],
                sum_send.at[g, e],
                sum_recv.at[g, e],
                "tp",
                lax.rem(tp + e, n_tp),
            )
            copy.start()
            sum_copies[g, e] = copy

    def expand(g):
        if g == 0:
            up_copy.wait()
        total = part_send[g]
        for e in range(1, n_tp):
            sum_copies[g, e].wait_recv()
            total = total + part_recv[g, e]
        turned = pltpu.roll(total, rank, 1)
        both = jnp.concatenate(
            [jnp.where(lane1 < rank, total, turned), jnp.where(lane1 < rank, turned, total)], axis=0
        )
        ids = ids_of(g) - part_of
        spread = jnp.concatenate(
            [jnp.where(ids == float(j * per), both, 0.0).astype(jnp.bfloat16) for j in range(pairs)],
            axis=1,
        )

        @pl.loop(0, columns // 256)
        def _(c):
            at = pl.ds(pl.multiple_of(c * 256, 256), 256)
            change = jnp.dot(spread, up_buf[:, at], preferred_element_type=jnp.float32)
            outgoing[pl.ds(2 * g, 2), :, at] = change.astype(jnp.bfloat16).reshape(2, cap, 256)

        for d in (2 * g, 2 * g + 1):
            if d:
                copy = remote(
                    outgoing.at[d],
                    returned.at[ad],
                    ret_send.at[d],
                    ret_recv.at[d],
                    "ad",
                    lax.rem(ad + n_ad - d, n_ad),
                )
                copy.start()
                ret_copies.append(copy)
            else:
                returned[ad] = outgoing[0]

    swap(0, keys_hbm, swap_keys)
    shrink(0)
    base_chunk(0)
    expand(0)
    for copy in cache_copies:
        copy.start()
    for g in range(1, groups):
        shrink(g)
        if g < n_tp:
            base_chunk(g)
        expand(g)
    swap(1, values_hbm, swap_values)
    for e in range(groups, n_tp):
        base_chunk(e)
    for copy in ret_copies:
        copy.wait_recv()

    @pl.loop(0, columns // 256)
    def _(c):
        at = pl.ds(pl.multiple_of(c * 256, 256), 256)
        delta = jnp.dot(
            unpack_ref[...],
            returned[:, :, at].reshape(n_ad * cap, 256),
            preferred_element_type=jnp.float32,
        )
        query = acc[:, at] + delta
        pieces = []
        for h in range(256 // size):
            one = query[:, h * size : (h + 1) * size]
            pieces.append(one * cos_ref[...] + pltpu.roll(one, size // 2, 1) * sin_ref[...])
        out_ref[:, at] = jnp.concatenate(pieces, axis=1).astype(jnp.bfloat16)

    for h in range(heads):
        heads_f32[:, h, :] = out_ref[:, h * size : (h + 1) * size].astype(jnp.float32)
    heads_bf16[...] = heads_f32[...].astype(jnp.bfloat16)

    sends = {}
    for c in range(chunks):
        for e in range(1, n_tp):
            copy = remote(
                heads_bf16.at[pl.ds(swapped + c * chunk, chunk)],
                every.at[tp, pl.ds(c * chunk, chunk)],
                q_send.at[c, e],
                q_recv.at[c, e],
                "tp",
                lax.rem(tp + e, n_tp),
            )
            copy.start()
            sends[c, e] = copy
    every[tp] = heads_bf16[pl.ds(swapped, spread_rows)]

    for copy in swap_copies:
        copy.wait_recv()
    for copy in cache_copies:
        copy.wait()

    own_head = lax.broadcasted_iota(jnp.int32, (heads, cells), 0) // (heads // kv_mine)
    own_cell = lax.broadcasted_iota(jnp.int32, (heads, cells), 1)
    block = kv_mine * span
    own_mine = own_head == (own_cell % block) // span
    source = lax.rem(tp + n_tp - own_cell // block, n_tp)
    own_position = jnp.where(own_mine, source * span + own_cell % span, 1 << 30)

    @pl.loop(0, swapped // 8)
    def _(b):
        for u in range(8):
            r = b * 8 + u
            score = (
                lax.dot_general(
                    heads_bf16[r],
                    swap_keys[r].reshape(cells, size),
                    (((1,), (1,)), ((), ())),
                    preferred_element_type=jnp.float32,
                )
                * scale
            )
            valid = own_position < lengths_ref[r]
            score = jnp.where(valid, score, -1e30)
            peak = jnp.max(score, axis=1, keepdims=True)
            weight = jnp.where(valid, jnp.exp(score - peak), 0.0)
            total = jnp.sum(weight, axis=1, keepdims=True)
            result = jnp.dot(
                weight.astype(jnp.bfloat16),
                swap_values[r].reshape(cells, size),
                preferred_element_type=jnp.float32,
            )
            heads_f32[r] = result / total

    head_of = lax.broadcasted_iota(jnp.int32, (all_heads, cells), 0) // (all_heads // kv_heads)
    cell = lax.broadcasted_iota(jnp.int32, (all_heads, cells), 1)
    mine = head_of == cell // span
    position = jnp.where(mine, tp * span + cell % span, 1 << 30)
    lane = lax.broadcasted_iota(jnp.int32, (all_heads, LANES), 1)
    lane_h = lax.broadcasted_iota(jnp.int32, (heads, LANES), 1)
    unroll = 4
    outs = []

    def attend(c):
        for e in range(1, n_tp):
            sends[c, e].wait_recv()

        def some(b, held):
            for u in range(unroll):
                local = b * unroll + u
                r = c * chunk + local
                query = jnp.concatenate([every[t, r] for t in range(n_tp)], axis=0)
                score = (
                    lax.dot_general(
                        query,
                        keys[r].reshape(cells, size),
                        (((1,), (1,)), ((), ())),
                        preferred_element_type=jnp.float32,
                    )
                    * scale
                )
                valid = position < lengths_ref[swapped + r]
                score = jnp.where(valid, score, -1e30)
                peak = jnp.max(score, axis=1, keepdims=True)
                weight = jnp.where(valid, jnp.exp(score - peak), 0.0)
                total = jnp.sum(weight, axis=1, keepdims=True)
                result = jnp.dot(
                    weight.astype(jnp.bfloat16),
                    values[r].reshape(cells, size),
                    preferred_element_type=jnp.float32,
                ).astype(jnp.bfloat16)
                for t in range(n_tp):
                    part[t, r] = result[t * heads : (t + 1) * heads]
                held = jnp.where(lane == local, peak, held)
                held = jnp.where(lane == local + LANES // 2, total, held)
            return held

        held = lax.fori_loop(
            0, chunk // unroll, some, jnp.zeros((all_heads, LANES), jnp.float32)
        )
        for t in range(n_tp):
            stat[c, t] = held[t * heads : (t + 1) * heads]
        at = pl.ds(c * chunk, chunk)
        for e in range(1, n_tp):
            peer = lax.rem(tp + e, n_tp)
            s = remote(
                stat.at[c, peer], stat_in.at[c, e], s_send.at[c, e], s_recv.at[c, e], "tp", peer
            )
            p = remote(
                part.at[peer, at], part_in.at[e, at], p_send.at[c, e], p_recv.at[c, e], "tp", peer
            )
            s.start()
            p.start()
            outs.append((c, s))
            outs.append((c, p))
        part_in[0, at] = part[tp, at]
        stat_in[c, 0] = stat[c, tp]

    def combine(c):
        for k, copy in outs:
            if k == c:
                copy.wait_recv()
        stats = [stat_in[c, e] for e in range(n_tp)]
        top = functools.reduce(jnp.maximum, stats)
        factors = [jnp.exp(s - top) for s in stats]
        denom = sum(f * pltpu.roll(s, LANES // 2, 1) for f, s in zip(factors, stats))
        shares = [f / denom for f in factors]

        @pl.loop(0, chunk // unroll)
        def _(b):
            for u in range(unroll):
                local = b * unroll + u
                r = c * chunk + local
                result = jnp.zeros((heads, size), jnp.float32)
                for e in range(n_tp):
                    share = jnp.sum(
                        jnp.where(lane_h == local, shares[e], 0.0), axis=1, keepdims=True
                    )
                    result = result + share * part_in[e, r].astype(jnp.float32)
                heads_f32[swapped + r] = result

    for c in range(chunks):
        attend(c)
        if c:
            combine(c - 1)
    combine(chunks - 1)
    for h in range(heads):
        att_ref[:, h * size : (h + 1) * size] = heads_f32[:, h, :].astype(jnp.bfloat16)

    for copy in row_copies + tok_copies + list(sum_copies.values()) + ret_copies:
        copy.wait_send()
    for copy in swap_copies + list(sends.values()) + [copy for _, copy in outs]:
        copy.wait_send()


def fused_device(
    tokens,
    query_weight,
    adapter_down_weight,
    adapter_up_weight,
    row_adapter_index,
    adapter_table_slot,
    lengths,
    cached_key_rows,
    cached_value_rows,
):
    rows, features = tokens.shape
    columns = query_weight.shape[1]
    n_ad = lax.axis_size("ad")
    n_tp = lax.axis_size("tp")
    held = adapter_down_weight.shape[0]
    rank = adapter_down_weight.shape[2]
    _, kv_heads, span, head_dim = cached_key_rows.shape
    cap = -(-(384 // n_ad) // 16) * 16

    slots = lookup(row_adapter_index, adapter_table_slot)
    owner = slots // held
    order = jnp.arange(rows, dtype=jnp.int32)
    before = (owner[:, None] == owner[None, :]) & (order[None, :] < order[:, None])
    place = owner * cap + jnp.sum(before.astype(jnp.int32), axis=1)
    cells = jnp.arange(n_ad * cap, dtype=jnp.int32)
    unpack = (place[:, None] == cells[None, :]).astype(jnp.bfloat16)
    mark = jnp.broadcast_to((slots % held + 1).astype(jnp.bfloat16)[:, None], (rows, LANES))

    half = head_dim // 2
    freq = jnp.exp(jnp.arange(half, dtype=jnp.float32) * (-2.0 * math.log(500000.0) / head_dim))
    angle = (lengths - 1).astype(jnp.float32)[:, None] * freq[None, :]
    cosine = jnp.cos(angle)
    sine = jnp.sin(angle)
    cos_full = jnp.concatenate([cosine, cosine], axis=1)
    sin_full = jnp.concatenate([-sine, sine], axis=1)

    depth = 1024
    slot_count = 4
    swapped = SWAPPED
    chunk = 32
    heads = columns // head_dim
    spread_rows = rows - swapped
    chunks = spread_rows // chunk
    kv_mine = kv_heads // n_tp
    vmem = pl.BlockSpec(memory_space=pltpu.VMEM)
    smem = pl.BlockSpec(memory_space=pltpu.SMEM)
    anywhere = pl.BlockSpec(memory_space=pl.ANY)
    bf16, f32 = jnp.bfloat16, jnp.float32
    dma = pltpu.SemaphoreType.DMA
    groups = n_ad // 2
    return pl.pallas_call(
        functools.partial(step_kernel, n_ad, n_tp, cap, rank, swapped, chunk),
        out_shape=(jax.ShapeDtypeStruct((rows, columns), bf16),) * 2,
        in_specs=[vmem] * 6 + [smem] + [anywhere] * 5,
        out_specs=(vmem, vmem),
        scratch_shapes=[
            pltpu.VMEM((n_ad, cap, features + LANES), bf16),
            pltpu.VMEM((n_tp, rows, features), bf16),
            pltpu.VMEM((n_ad, cap, features + LANES), bf16),
            pltpu.VMEM((n_ad, cap, columns), bf16),
            pltpu.VMEM((n_ad, cap, columns), bf16),
            pltpu.VMEM((groups, cap, LANES), f32),
            pltpu.VMEM((groups, n_tp, cap, LANES), f32),
            pltpu.VMEM((rows, columns), f32),
            pltpu.VMEM((slot_count, depth, columns), bf16),
            pltpu.VMEM((held * rank, features), bf16),
            pltpu.VMEM((held * rank, columns), bf16),
            pltpu.VMEM((rows, heads, head_dim), f32),
            pltpu.VMEM((rows, heads, head_dim), bf16),
            pltpu.VMEM((swapped, n_tp, kv_mine, span, head_dim), bf16),
            pltpu.VMEM((swapped, n_tp, kv_mine, span, head_dim), bf16),
            pltpu.VMEM((n_tp, spread_rows, heads, head_dim), bf16),
            pltpu.VMEM((spread_rows, kv_heads, span, head_dim), bf16),
            pltpu.VMEM((spread_rows, kv_heads, span, head_dim), bf16),
            pltpu.VMEM((n_tp, spread_rows, heads, head_dim), bf16),
            pltpu.VMEM((chunks, n_tp, heads, LANES), f32),
            pltpu.VMEM((n_tp, spread_rows, heads, head_dim), bf16),
            pltpu.VMEM((chunks, n_tp, heads, LANES), f32),
            dma((slot_count,)),
            dma((6,)),
            dma((n_tp,)),
            dma((n_tp,)),
            dma((n_ad,)),
            dma((n_ad,)),
            dma((groups, n_tp)),
            dma((groups, n_tp)),
            dma((n_ad,)),
            dma((n_ad,)),
            dma((2, n_tp)),
            dma((2, n_tp)),
            dma((chunks, n_tp)),
            dma((chunks, n_tp)),
            dma((chunks, n_tp)),
            dma((chunks, n_tp)),
            dma((chunks, n_tp)),
            dma((chunks, n_tp)),
        ],
        compiler_params=pltpu.CompilerParams(
            collective_id=0, has_side_effects=True, vmem_limit_bytes=60 * 1024 * 1024
        ),
        name="step",
    )(
        place[None, :],
        mark,
        unpack,
        tokens,
        cos_full,
        sin_full,
        lengths,
        query_weight,
        adapter_down_weight.transpose(0, 2, 1).reshape(held * rank, features),
        adapter_up_weight.reshape(held * rank, columns),
        cached_key_rows,
        cached_value_rows,
    )


def rotate(query, lengths):
    head_dim = query.shape[-1]
    half = head_dim // 2
    freq = jnp.exp(jnp.arange(half, dtype=jnp.float32) * (-2.0 * math.log(500000.0) / head_dim))
    angle = (lengths - 1).astype(jnp.float32)[:, None, None] * freq[None, None, :]
    cosine = jnp.cos(angle)
    sine = jnp.sin(angle)
    first = query[..., :half]
    second = query[..., half:]
    return jnp.concatenate(
        [first * cosine - second * sine, second * cosine + first * sine], axis=-1
    )


def lookup(ids, adapter_table_slot):
    table = jnp.arange(adapter_table_slot.shape[0], dtype=jnp.int32)
    return jnp.sum(
        jnp.where(ids[:, None] == table[None, :], adapter_table_slot[None, :], 0), axis=1
    )


def shrink_rows(input_rows, local_partial, adapter_down_weight):
    adapter_row_count = adapter_down_weight.shape[0]
    select_rows = (
        local_partial[:, None] == jnp.arange(adapter_row_count, dtype=jnp.int32)[None, :]
    ).astype(jnp.float32)
    update_terms = jnp.einsum(
        "nt,vtm->nvm", input_rows, adapter_down_weight, preferred_element_type=jnp.float32
    )
    return (select_rows, jnp.sum(update_terms * select_rows[:, :, None], axis=1))


def expand_rows(select_rows, reduced_rows, adapter_up_weight):
    spread_rows = (select_rows[:, :, None] * reduced_rows.astype(jnp.float32)[:, None, :]).astype(
        jnp.bfloat16
    )
    return jnp.einsum(
        "pow,owu->pu", spread_rows, adapter_up_weight, preferred_element_type=jnp.float32
    ).astype(jnp.bfloat16)


def per_device(
    tokens,
    query_weight,
    adapter_down_weight,
    adapter_up_weight,
    row_adapter_index,
    adapter_table_slot,
    lengths,
    cached_key_rows,
    cached_value_rows,
):
    rows = tokens.shape[0]
    columns = query_weight.shape[1]
    tp_count = lax.axis_size("tp")
    owner_partials = adapter_down_weight.shape[0]
    base = jnp.dot(
        lax.all_gather(tokens, "tp", axis=1, tiled=True),
        query_weight,
        preferred_element_type=jnp.float32,
    )
    combined_output, every_id = (
        lax.all_gather(tokens, "ad", axis=0, tiled=True),
        lax.all_gather(row_adapter_index, "ad", axis=0, tiled=True),
    )
    slots = lookup(every_id, adapter_table_slot)
    mine = slots // owner_partials == lax.axis_index("ad")
    local_partial = jnp.where(mine, slots % owner_partials, -1)
    select_rows, partial_value_sum = shrink_rows(
        combined_output, local_partial, adapter_down_weight
    )
    reduced_rows = lax.psum(partial_value_sum, "tp").astype(jnp.bfloat16)
    lowrank_change = expand_rows(select_rows, reduced_rows, adapter_up_weight)
    delta = lax.psum_scatter(
        lowrank_change.astype(jnp.float32).astype(jnp.bfloat16),
        "ad",
        scatter_dimension=0,
        tiled=True,
    ).astype(jnp.float32)
    head_dim = cached_key_rows.shape[3]
    query = (base + delta).reshape(rows, columns // head_dim, head_dim)
    queries = rotate(query, lengths).reshape(rows, columns).astype(jnp.bfloat16)
    every_head = lax.all_gather(queries, "tp", axis=1, tiled=True)
    kv_heads = cached_key_rows.shape[1]
    span = cached_key_rows.shape[2]
    grouped = every_head.reshape(rows, kv_heads, -1, head_dim)
    scores = jnp.einsum(
        "rkgd,rkpd->rkgp", grouped, cached_key_rows, preferred_element_type=jnp.float32
    ) * (1.0 / math.sqrt(head_dim))
    position = lax.axis_index("tp") * span + jnp.arange(span, dtype=jnp.int32)
    valid = (position[None, :] < lengths[:, None])[:, None, None, :]
    scores = jnp.where(valid, scores, -1e30)
    peak = jnp.max(scores, axis=-1)
    weights = jnp.where(valid, jnp.exp(scores - peak[..., None]), 0.0)
    total = jnp.sum(weights, axis=-1)
    partial_out = jnp.einsum(
        "rkgp,rkpd->rkgd",
        weights.astype(jnp.bfloat16),
        cached_value_rows,
        preferred_element_type=jnp.float32,
    ).astype(jnp.bfloat16)
    peaks, totals = (
        lax.all_to_all(
            peak.reshape(rows, tp_count, -1), "tp", split_axis=1, concat_axis=1, tiled=True
        ),
        lax.all_to_all(
            total.reshape(rows, tp_count, -1), "tp", split_axis=1, concat_axis=1, tiled=True
        ),
    )
    partials = lax.all_to_all(
        partial_out.reshape(rows, tp_count, -1), "tp", split_axis=1, concat_axis=1, tiled=True
    )
    highest = jnp.max(peaks, axis=1, keepdims=True)
    factor = jnp.exp(peaks - highest)
    numer = jnp.sum(
        factor[..., None] * partials.reshape(rows, tp_count, -1, head_dim).astype(jnp.float32),
        axis=1,
    )
    denom = jnp.sum(factor * totals, axis=1)
    attended = (numer / denom[..., None]).reshape(rows, columns).astype(jnp.bfloat16)
    return (queries, attended)


def solution(mesh):
    fits = mesh.shape["tp"] <= 4 and mesh.shape["ad"] % 2 == 0
    return jax.shard_map(
        fused_device if fits else per_device,
        mesh=mesh,
        in_specs=(
            P("ad", "tp"),
            P(None, "tp"),
            P("ad", "tp", None),
            P("ad", None, "tp"),
            P("ad"),
            P(),
            P("ad"),
            P("ad", None, "tp", None),
            P("ad", None, "tp", None),
        ),
        out_specs=(P("ad", "tp"), P("ad", "tp")),
        check_vma=False,
    )
```
